32 devices in a mesh: tm: 4 (over z), dom: 8 (over y, x, core).
Axes of the slice: x: 2, y: 2, z: 4, core: 2. Of those that a mesh axis runs over, the one named last changes fastest.
Arguments:
- video_group: bfloat16 [2, 16, 112, 128, 128], P(None, 'tm', 'dom'), may hold values from -6 to 6
- pairing: int32 [4, 2], P('tm'), may hold values from 0 to 1, each once within a row
- weight_one: bfloat16 [3, 3, 3, 128, 128], replicated, may hold values from -0.109375 to 0.109375
- weight_down: bfloat16 [3, 3, 128, 256], replicated, may hold values from -0.1875 to 0.1875
- weight_two: bfloat16 [3, 3, 3, 256, 256], replicated, may hold values from -0.078125 to 0.078125
Outputs:
- encoded: bfloat16 [2, 16, 56, 64, 256], P(None, 'tm', 'dom')
The draws below stay inside these ranges and needn't reach their ends.
Inputs may be any that keep to these rules, and one draw needn't show every extreme that they name: Each row of pairing names every clip slot exactly once.
All inputs are finite; a program needn't handle non-finite values.
Results may differ from the reference program's by a relative error of at most 0.008.
Values may be sent and summed in bfloat16 or wider, within the bound.
A program may use at most 128 MiB of HBM per device.

```python
import jax
import jax.numpy as jnp
from jax import lax

CH1 = 128
CH2 = 256
CLIPS = 2
TC = 4
W = 128
FRAMES = 16
H = 112
N_TM = 4


def block_scale(own_key, extent, split, least, top_value):
    level, own = 1.0, jax.random.fold_in(own_key, 6)
    for dim, shards_of in split:
        heights = jnp.exp(jax.random.uniform(jax.random.fold_in(own, dim), (shards_of,), jnp.float32, least / len(split), top_value / len(split)))
        level = level * jnp.repeat(heights, extent[dim] // shards_of).reshape([-1 if axis == dim else 1 for axis in range(len(extent))])
    return level


def scatter_about(rng, shape, width, limit, shards=(), dtype=jnp.bfloat16):
    array = width * jax.random.normal(rng, shape, jnp.float32)
    if shards:
        array = array * block_scale(rng, shape, shards, -0.22, 0.18)
    return jnp.clip(array, -limit, limit).astype(dtype)


def setup_inputs(seed: int = 0) -> dict:
    keys = jax.random.split(jax.random.key(seed), 6)
    return {
        "video_group": scatter_about(keys[0], (CLIPS, FRAMES, H, W, CH1), 1.0, 6.0, ((1, 4), (2, 8))),
        "pairing": jax.vmap(lambda own: jax.random.permutation(own, CLIPS))(jax.random.split(keys[1], N_TM)).reshape((N_TM, CLIPS)).astype(jnp.int32),
        "weight_one": scatter_about(keys[2], (3, 3, 3, CH1, CH1), (27 * CH1) ** -0.5, 0.109375),
        "weight_down": scatter_about(keys[3], (3, 3, CH1, CH2), (9 * CH1) ** -0.5, 0.1875),
        "weight_two": scatter_about(keys[4], (3, 3, 3, CH2, CH2), (27 * CH2) ** -0.5, 0.078125),
    }


LAYOUT = ("NDHWC", "DHWIO", "NDHWC")


def convolve(source, weight, pad_rows, pad_cols, stride):
    return lax.conv_general_dilated(source.astype(jnp.float32), weight.astype(jnp.float32), stride,
                                    [(0, 0), pad_rows, pad_cols], dimension_numbers=LAYOUT)


def causal_section(activated, residual_in, pairing, weight, group_len):
    outputs = []
    for group in range(N_TM):
        current = activated[:, group * group_len:(group + 1) * group_len]
        if group == 0:
            earlier = jnp.zeros_like(current[:, :2])
        else:
            earlier = jnp.take(activated[:, group * group_len - 2:group * group_len], pairing[group].astype(jnp.int32), axis=0)
        extended = jnp.concatenate([earlier, current], axis=1)
        summed = convolve(extended, weight, (1, 1), (1, 1), (1, 1, 1))
        skipped = residual_in[:, group * group_len:(group + 1) * group_len].astype(jnp.float32)
        outputs.append((skipped + summed).astype(jnp.bfloat16))
    return jnp.concatenate(outputs, axis=1)


def reference(video_group, pairing, weight_one, weight_down, weight_two):
    activated = jax.nn.silu(video_group.astype(jnp.float32)).astype(jnp.bfloat16)
    hidden = causal_section(activated, video_group, pairing, weight_one, TC)
    reduced = convolve(hidden, weight_down[None], (0, 1), (0, 1), (1, 2, 2)).astype(jnp.bfloat16)
    gated_act = jax.nn.silu(reduced.astype(jnp.float32)).astype(jnp.bfloat16)
    return causal_section(gated_act, reduced, pairing, weight_two, TC)
```

```python
import functools

import jax
import jax.numpy as jnp
from jax import lax
from jax.experimental import pallas as pl
from jax.experimental.pallas import tpu as pltpu
from jax.sharding import PartitionSpec as P

MESH = pl.DeviceIdType.MESH
F32, BF16 = jnp.float32, jnp.bfloat16


def silu(v):
    half = 0.5 * v
    return half + half * jnp.tanh(half)


def chunk_rows(rows, width, limit):
    return max(d for d in range(1, rows + 1) if rows % d == 0 and (d == 1 or d * width <= limit))


def kernel(
    n_tm, n_dom,
    video, pairing, weight_one, weight_down, weight_two, out,
    vbuf, arr0, arr1, x4, resid, w1, wd, w2, stage, stage_raw, h3, stage_h,
    red, gbuf, garr0, garr1, g3, stage_g, obuf,
    local_sem, send_sem, recv_sem,
):
    slots, frames, rows, width, ch1 = video.shape
    rows2, cols2, ch2 = rows // 2, width // 2, out.shape[-1]
    tm, dom = lax.axis_index("tm"), lax.axis_index("dom")
    arr, garr = (arr0, arr1), (garr0, garr1)
    has_prev, has_next = tm > 0, tm < n_tm - 1
    has_up, has_down = dom > 0, dom < n_dom - 1
    prev, nxt, up, down = (tm - 1, dom), (tm + 1, dom), (tm, dom - 1), (tm, dom + 1)

    loads = [
        pltpu.make_async_copy(video, vbuf.at[:, :, 1 : rows + 1], local_sem.at[0]),
        pltpu.make_async_copy(weight_one, w1.at[:, 0 : 3 * ch1, 0:ch1], local_sem.at[1]),
        pltpu.make_async_copy(weight_one, w1.at[:, ch1 : 4 * ch1, ch1 : 2 * ch1], local_sem.at[2]),
        pltpu.make_async_copy(weight_down, wd, local_sem.at[3]),
        pltpu.make_async_copy(weight_two, w2, local_sem.at[4]),
    ]
    for load in loads:
        load.start()

    barrier = pltpu.get_barrier_semaphore()
    for there, device in ((has_prev, prev), (has_next, nxt), (has_up, up), (has_down, down)):
        @pl.when(there)
        def _():
            pl.semaphore_signal(barrier, inc=1, device_id=device, device_id_type=MESH)
    peers = sum(there.astype(jnp.int32) for there in (has_prev, has_next, has_up, has_down))
    pl.semaphore_wait(barrier, peers)

    counter = [0]

    def remote(src, dst, device, sends, receives):
        index = counter[0]
        counter[0] += 1
        copy = pltpu.make_async_remote_copy(
            src_ref=src, dst_ref=dst, send_sem=send_sem.at[index], recv_sem=recv_sem.at[index],
            device_id=device, device_id_type=MESH,
        )
        sent.append((copy, sends))
        return copy, sends, receives

    sent = []

    def start(item):
        @pl.when(item[1])
        def _():
            item[0].start()

    def arrive(item):
        @pl.when(item[2])
        def _():
            item[0].wait_recv()

    frame_moves = [
        remote(video.at[:, frames - 2 + e], arr[e].at[:, 1 : rows + 1], nxt, has_next, has_prev)
        for e in (0, 1)
    ]
    own_rows = [
        remote(video.at[:, :, 0:2], vbuf.at[:, :, rows + 1 : rows + 3], up, has_up, has_down),
        remote(video.at[:, :, rows - 1 : rows], vbuf.at[:, :, 0:1], down, has_down, has_up),
    ]
    relay_up, relay_down = has_prev & has_up, has_prev & has_down
    frame_rows = [
        [
            remote(arr[e].at[:, 1:3], arr[e].at[:, rows + 1 : rows + 3], up, relay_up, relay_down),
            remote(arr[e].at[:, rows : rows + 1], arr[e].at[:, 0:1], down, relay_down, relay_up),
        ]
        for e in (0, 1)
    ]
    gated_moves = [
        remote(
            gbuf.at[frames - 2 + e, :, 1 : rows2 + 1], garr[e].at[:, 1 : rows2 + 1],
            nxt, has_next, has_prev,
        )
        for e in (0, 1)
    ]
    gated_rows = [
        [
            remote(gbuf.at[f, :, 1:2], gbuf.at[f, :, rows2 + 1 : rows2 + 2], up, has_up, has_down),
            remote(gbuf.at[f, :, rows2 : rows2 + 1], gbuf.at[f, :, 0:1], down, has_down, has_up),
        ]
        for f in range(frames)
    ]
    gated_frame_rows = [
        [
            remote(garr[e].at[:, 1:2], garr[e].at[:, rows2 + 1 : rows2 + 2], up, relay_up, relay_down),
            remote(garr[e].at[:, rows2 : rows2 + 1], garr[e].at[:, 0:1], down, relay_down, relay_up),
        ]
        for e in (0, 1)
    ]

    for item in own_rows:
        start(item)
    start(frame_moves[1])
    start(frame_moves[0])

    w1[:, 3 * ch1 : 4 * ch1, 0:ch1] = jnp.zeros((w1.shape[0], ch1, ch1), BF16)
    w1[:, 0:ch1, ch1 : 2 * ch1] = jnp.zeros((w1.shape[0], ch1, ch1), BF16)
    stage[:, 0:8] = jnp.zeros((rows + 3, 8, ch1), F32)
    stage[:, width + 8 : width + 16] = jnp.zeros((rows + 3, 8, ch1), F32)
    stage_h[:, cols2 : cols2 + 8] = jnp.zeros((stage_h.shape[0], 8, ch1), F32)
    stage_g[:, 0:8] = jnp.zeros((rows2 + 2, 8, ch2), F32)
    stage_g[:, cols2 + 8 : cols2 + 16] = jnp.zeros((rows2 + 2, 8, ch2), F32)

    @pl.when(jnp.logical_not(has_up))
    def _():
        vbuf[:, :, 0:1] = jnp.zeros((slots, frames, 1, width, ch1), BF16)
        gbuf[:, :, 0:1] = jnp.zeros((frames, slots, 1, cols2, ch2), BF16)
        for e in (0, 1):
            arr[e][:, 0:1] = jnp.zeros((slots, 1, width, ch1), BF16)
            garr[e][:, 0:1] = jnp.zeros((slots, 1, cols2, ch2), BF16)

    @pl.when(jnp.logical_not(has_down))
    def _():
        vbuf[:, :, rows + 1 : rows + 3] = jnp.zeros((slots, frames, 2, width, ch1), BF16)
        gbuf[:, :, rows2 + 1 : rows2 + 2] = jnp.zeros((frames, slots, 1, cols2, ch2), BF16)
        for e in (0, 1):
            arr[e][:, rows + 1 : rows + 3] = jnp.zeros((slots, 2, width, ch1), BF16)
            garr[e][:, rows2 + 1 : rows2 + 2] = jnp.zeros((slots, 1, cols2, ch2), BF16)

    def spread_activated(source, s, e):
        def one(r, carry):
            v = source(r).astype(F32)
            stage[r, 8 : width + 8] = silu(v)
            for c in range(4):
                part = stage[r, pl.ds(7 + c, cols2, stride=2), :]
                x4[s, e, r, :, c * ch1 : (c + 1) * ch1] = part.astype(BF16)
            return carry

        lax.fori_loop(0, rows + 3, one, 0, unroll=2)

    def spread_own(f):
        def slot(s, carry):
            spread_activated(lambda r: vbuf[s, f, r], s, f + 2)

            def one(r, inner):
                stage_raw[r] = vbuf[s, f, r + 1].astype(F32)
                for c in range(2):
                    part = stage_raw[r, pl.ds(c, cols2, stride=2), :]
                    resid[s, f, r, :, c * ch1 : (c + 1) * ch1] = part.astype(BF16)
                return inner

            lax.fori_loop(0, rows + 1, one, 0, unroll=2)
            return carry

        lax.fori_loop(0, slots, slot, 0)

    def spread_arrived(e):
        @pl.when(has_prev)
        def _():
            def slot(s, carry):
                source_slot = pairing[0, s]
                spread_activated(lambda r: arr[e][source_slot, r], s, e)
                return carry

            lax.fori_loop(0, slots, slot, 0)

        @pl.when(jnp.logical_not(has_prev))
        def _():
            x4[:, e] = jnp.zeros((slots, rows + 3, cols2, 4 * ch1), BF16)

    step = chunk_rows(rows + 1, cols2, 512)
    chunks = (rows + 1) // step

    def first_section(f):
        def slot(s, carry):
            def chunk(i, inner):
                first = i * step
                taps = [
                    x4[s, f + kf, pl.ds(first + kr, step)].reshape(step * cols2, 4 * ch1)
                    for kf in range(3) for kr in range(3)
                ]
                acc = jnp.dot(
                    jnp.concatenate(taps, axis=1), w1[...].reshape(-1, 2 * ch1),
                    preferred_element_type=F32,
                ).reshape(step, cols2, 2 * ch1)
                acc = acc + resid[s, f, pl.ds(first, step)].astype(F32)
                row = first + lax.broadcasted_iota(jnp.int32, (step, 1, 1), 0)
                keep = (row < rows) | has_down
                acc = jnp.where(keep, acc, 0.0)
                stage_h[:, 0:cols2] = acc[:, :, 0:ch1]
                h3[pl.ds(first, step), :, 0 : 2 * ch1] = acc.astype(BF16)
                h3[pl.ds(first, step), :, 2 * ch1 : 3 * ch1] = stage_h[:, 1 : cols2 + 1].astype(BF16)
                return inner

            lax.fori_loop(0, chunks, chunk, 0)
            taps = [
                jnp.concatenate([h3[2 * i + p] for i in range(rows2)], axis=0) for p in range(3)
            ]
            value = jnp.dot(
                jnp.concatenate(taps, axis=1), wd[...].reshape(-1, ch2), preferred_element_type=F32
            ).astype(BF16).reshape(rows2, cols2, ch2)
            red[f, s] = value
            gbuf[f, s, 1 : rows2 + 1] = silu(value.astype(F32)).astype(BF16)
            return carry

        lax.fori_loop(0, slots, slot, 0)

    def spread_gated(source, s, e):
        v = source
        wide = v.astype(F32)
        stage_g[:, 8 : cols2 + 8] = wide
        g3[s, e, :, :, ch2 : 2 * ch2] = v
        g3[s, e, :, :, 0:ch2] = stage_g[:, 7 : cols2 + 7].astype(BF16)
        g3[s, e, :, :, 2 * ch2 : 3 * ch2] = stage_g[:, 9 : cols2 + 9].astype(BF16)

    def spread_gated_own(f):
        def slot(s, carry):
            spread_gated(gbuf[f, s], s, f + 2)
            return carry

        lax.fori_loop(0, slots, slot, 0)

    def spread_gated_arrived(e):
        @pl.when(has_prev)
        def _():
            def slot(s, carry):
                spread_gated(garr[e][pairing[0, s]], s, e)
                return carry

            lax.fori_loop(0, slots, slot, 0)

        @pl.when(jnp.logical_not(has_prev))
        def _():
            g3[:, e] = jnp.zeros((slots, rows2 + 2, cols2, 3 * ch2), BF16)

    stores = [
        pltpu.make_async_copy(obuf.at[f], out.at[:, f], local_sem.at[5 + f]) for f in range(frames)
    ]

    def second_section(f):
        def slot(s, carry):
            taps = [
                g3[s, f + kf, kr : kr + rows2].reshape(rows2 * cols2, 3 * ch2)
                for kf in range(3) for kr in range(3)
            ]
            acc = jnp.dot(
                jnp.concatenate(taps, axis=1), w2[...].reshape(-1, ch2), preferred_element_type=F32
            ).reshape(rows2, cols2, ch2)
            obuf[f, s] = (red[f, s].astype(F32) + acc).astype(BF16)
            return carry

        lax.fori_loop(0, slots, slot, 0)
        stores[f].start()

    def arrive_and_relay(move, row_moves):
        arrive(move)
        for item in row_moves:
            start(item)

    loads[0].wait()
    for item in own_rows:
        arrive(item)
    for f in range(frames):
        spread_own(f)
    for load in loads[1:4]:
        load.wait()
    for f in range(frames - 1, 1, -1):
        first_section(f)
        for item in gated_rows[f]:
            start(item)
        if f >= frames - 2:
            start(gated_moves[f - frames + 2])
    arrive_and_relay(frame_moves[1], frame_rows[1])
    for f in range(frames - 1, 1, -1):
        for item in gated_rows[f]:
            arrive(item)
        spread_gated_own(f)
    for item in frame_rows[1]:
        arrive(item)
    spread_arrived(1)
    first_section(1)
    for item in gated_rows[1]:
        start(item)
    loads[4].wait()
    for f in range(frames - 1, 3, -1):
        second_section(f)
    for item in gated_rows[1]:
        arrive(item)
    spread_gated_own(1)
    second_section(3)
    arrive_and_relay(frame_moves[0], frame_rows[0])
    for item in frame_rows[0]:
        arrive(item)
    spread_arrived(0)
    first_section(0)
    for item in gated_rows[0]:
        start(item)
    arrive_and_relay(gated_moves[1], gated_frame_rows[1])
    for item in gated_rows[0]:
        arrive(item)
    spread_gated_own(0)
    second_section(2)
    for item in gated_frame_rows[1]:
        arrive(item)
    spread_gated_arrived(1)
    second_section(1)
    arrive_and_relay(gated_moves[0], gated_frame_rows[0])
    for item in gated_frame_rows[0]:
        arrive(item)
    spread_gated_arrived(0)
    second_section(0)
    for copy, sends in sent:
        @pl.when(sends)
        def _():
            copy.wait_send()
    for store in stores:
        store.wait()


def on_device(n_tm, n_dom, video_group, pairing, weight_one, weight_down, weight_two):
    slots, frames, rows, width, ch1 = video_group.shape
    ch2 = weight_two.shape[-1]
    rows2, cols2 = rows // 2, width // 2
    step = chunk_rows(rows + 1, cols2, 512)
    any_spec = pl.BlockSpec(memory_space=pl.ANY)
    copies = 2 + 2 + 4 + 2 + 2 * frames + 4
    return pl.pallas_call(
        functools.partial(kernel, n_tm, n_dom),
        out_shape=jax.ShapeDtypeStruct((slots, frames, rows2, cols2, ch2), BF16),
        in_specs=[any_spec, pl.BlockSpec(memory_space=pltpu.SMEM), any_spec, any_spec, any_spec],
        out_specs=any_spec,
        scratch_shapes=[
            pltpu.VMEM((slots, frames, rows + 3, width, ch1), BF16),
            pltpu.VMEM((slots, rows + 3, width, ch1), BF16),
            pltpu.VMEM((slots, rows + 3, width, ch1), BF16),
            pltpu.VMEM((slots, frames + 2, rows + 3, cols2, 4 * ch1), BF16),
            pltpu.VMEM((slots, frames, rows + 1, cols2, 2 * ch1), BF16),
            pltpu.VMEM((9, 4 * ch1, 2 * ch1), BF16),
            pltpu.VMEM((3, 3 * ch1, ch2), BF16),
            pltpu.VMEM((9, 3 * ch2, ch2), BF16),
            pltpu.VMEM((rows + 3, width + 16, ch1), F32),
            pltpu.VMEM((rows + 1, width, ch1), F32),
            pltpu.VMEM((rows + 1, cols2, 3 * ch1), BF16),
            pltpu.VMEM((step, cols2 + 8, ch1), F32),
            pltpu.VMEM((frames, slots, rows2, cols2, ch2), BF16),
            pltpu.VMEM((frames, slots, rows2 + 2, cols2, ch2), BF16),
            pltpu.VMEM((slots, rows2 + 2, cols2, ch2), BF16),
            pltpu.VMEM((slots, rows2 + 2, cols2, ch2), BF16),
            pltpu.VMEM((slots, frames + 2, rows2 + 2, cols2, 3 * ch2), BF16),
            pltpu.VMEM((rows2 + 2, cols2 + 16, ch2), F32),
            pltpu.VMEM((frames, slots, rows2, cols2, ch2), BF16),
            pltpu.SemaphoreType.DMA((5 + frames,)),
            pltpu.SemaphoreType.DMA((copies,)),
            pltpu.SemaphoreType.DMA((copies,)),
        ],
        compiler_params=pltpu.CompilerParams(
            collective_id=0, has_side_effects=True, vmem_limit_bytes=63 * 1024 * 1024
        ),
        name="block",
    )(
        video_group,
        pairing,
        weight_one.reshape(9, 3 * ch1, ch1),
        weight_down.reshape(3, 3 * ch1, ch2),
        weight_two.reshape(9, 3 * ch2, ch2),
    )


def solution(mesh):
    return jax.shard_map(
        functools.partial(on_device, mesh.shape["tm"], mesh.shape["dom"]),
        mesh=mesh,
        in_specs=(P(None, "tm", "dom", None, None), P("tm", None), P(), P(), P()),
        out_specs=P(None, "tm", "dom", None, None),
        check_vma=False,
    )
```

```python
import functools

import jax
import jax.numpy as jnp
from jax import lax
from jax.experimental import pallas as pl
from jax.experimental.pallas import tpu as pltpu
from jax.sharding import PartitionSpec as P

MESH = pl.DeviceIdType.MESH
F32, BF16 = jnp.float32, jnp.bfloat16


def silu(v):
    half = 0.5 * v
    return half + half * jnp.tanh(half)


def chunk_rows(rows, width, limit):
    return max(d for d in range(1, rows + 1) if rows % d == 0 and (d == 1 or d * width <= limit))


def kernel(
    n_tm, n_dom,
    video, pairing, weight_one, weight_down, weight_two, out,
    vbuf, x4, resid, w1, wd, w2, stage, stage_raw, h3, stage_h,
    red, gbuf, g3, stage_g, obuf, oacc, pbuf, parr0, parr1, qbuf, qarr0, qarr1,
    local_sem, send_sem, recv_sem,
):
    slots, frames, rows, width, ch1 = video.shape
    rows2, cols2, ch2 = rows // 2, width // 2, out.shape[-1]
    tm, dom = lax.axis_index("tm"), lax.axis_index("dom")
    parr, qarr = (parr0, parr1), (qarr0, qarr1)
    has_prev, has_next = tm > 0, tm < n_tm - 1
    has_up, has_down = dom > 0, dom < n_dom - 1
    prev, nxt, up, down = (tm - 1, dom), (tm + 1, dom), (tm, dom - 1), (tm, dom + 1)

    loads = [
        pltpu.make_async_copy(video, vbuf.at[:, :, 1 : rows + 1], local_sem.at[0]),
        pltpu.make_async_copy(weight_one, w1.at[:, 0 : 3 * ch1, 0:ch1], local_sem.at[1]),
        pltpu.make_async_copy(weight_one, w1.at[:, ch1 : 4 * ch1, ch1 : 2 * ch1], local_sem.at[2]),
        pltpu.make_async_copy(weight_down, wd, local_sem.at[3]),
        pltpu.make_async_copy(weight_two, w2, local_sem.at[4]),
    ]
    for load in loads:
        load.start()

    barrier = pltpu.get_barrier_semaphore()
    for there, device in ((has_prev, prev), (has_next, nxt), (has_up, up), (has_down, down)):
        @pl.when(there)
        def _():
            pl.semaphore_signal(barrier, inc=1, device_id=device, device_id_type=MESH)
    peers = sum(there.astype(jnp.int32) for there in (has_prev, has_next, has_up, has_down))
    pl.semaphore_wait(barrier, peers)

    sent = []

    def remote(src, dst, device, sends, receives):
        index = len(sent)
        copy = pltpu.make_async_remote_copy(
            src_ref=src, dst_ref=dst, send_sem=send_sem.at[index], recv_sem=recv_sem.at[index],
            device_id=device, device_id_type=MESH,
        )
        sent.append((copy, sends))
        return copy, sends, receives

    def start(item):
        @pl.when(item[1])
        def _():
            item[0].start()

    def arrive(item):
        @pl.when(item[2])
        def _():
            item[0].wait_recv()

    own_rows = [
        remote(video.at[:, :, 0:2], vbuf.at[:, :, rows + 1 : rows + 3], up, has_up, has_down),
        remote(video.at[:, :, rows - 1 : rows], vbuf.at[:, :, 0:1], down, has_down, has_up),
    ]
    gated_rows = [
        [
            remote(gbuf.at[f, :, 1:2], gbuf.at[f, :, rows2 + 1 : rows2 + 2], up, has_up, has_down),
            remote(gbuf.at[f, :, rows2 : rows2 + 1], gbuf.at[f, :, 0:1], down, has_down, has_up),
        ]
        for f in range(frames)
    ]
    first_moves = [remote(pbuf.at[e], parr[e], nxt, has_next, has_prev) for e in (0, 1)]
    second_moves = [remote(qbuf.at[e], qarr[e], nxt, has_next, has_prev) for e in (0, 1)]

    for item in own_rows:
        start(item)

    w1[:, 3 * ch1 : 4 * ch1, 0:ch1] = jnp.zeros((w1.shape[0], ch1, ch1), BF16)
    w1[:, 0:ch1, ch1 : 2 * ch1] = jnp.zeros((w1.shape[0], ch1, ch1), BF16)
    stage[:, 0:8] = jnp.zeros((rows + 3, 8, ch1), F32)
    stage[:, width + 8 : width + 16] = jnp.zeros((rows + 3, 8, ch1), F32)
    stage_h[:, cols2 : cols2 + 8] = jnp.zeros((stage_h.shape[0], 8, ch1), F32)
    stage_g[:, 0:8] = jnp.zeros((rows2 + 2, 8, ch2), F32)
    stage_g[:, cols2 + 8 : cols2 + 16] = jnp.zeros((rows2 + 2, 8, ch2), F32)

    @pl.when(jnp.logical_not(has_up))
    def _():
        vbuf[:, :, 0:1] = jnp.zeros((slots, frames, 1, width, ch1), BF16)
        gbuf[:, :, 0:1] = jnp.zeros((frames, slots, 1, cols2, ch2), BF16)

    @pl.when(jnp.logical_not(has_down))
    def _():
        vbuf[:, :, rows + 1 : rows + 3] = jnp.zeros((slots, frames, 2, width, ch1), BF16)
        gbuf[:, :, rows2 + 1 : rows2 + 2] = jnp.zeros((frames, slots, 1, cols2, ch2), BF16)

    @pl.when(jnp.logical_not(has_prev))
    def _():
        for e in (0, 1):
            parr[e][...] = jnp.zeros(parr[e].shape, BF16)
            qarr[e][...] = jnp.zeros(qarr[e].shape, BF16)

    def each_slot(body):
        def slot(s, carry):
            body(s)
            return carry

        lax.fori_loop(0, slots, slot, 0)

    def spread_own(f):
        def slot(s):
            def activated(r, inner):
                stage[r, 8 : width + 8] = silu(vbuf[s, f, r].astype(F32))
                for c in range(4):
                    part = stage[r, pl.ds(7 + c, cols2, stride=2), :]
                    x4[s, f, r, :, c * ch1 : (c + 1) * ch1] = part.astype(BF16)
                return inner

            lax.fori_loop(0, rows + 3, activated, 0, unroll=2)

            def raw(r, inner):
                stage_raw[r] = vbuf[s, f, r + 1].astype(F32)
                for c in range(2):
                    part = stage_raw[r, pl.ds(c, cols2, stride=2), :]
                    resid[s, f, r, :, c * ch1 : (c + 1) * ch1] = part.astype(BF16)
                return inner

            lax.fori_loop(0, rows + 1, raw, 0, unroll=2)

        each_slot(slot)

    step = chunk_rows(rows + 1, cols2, 512)
    chunks = (rows + 1) // step

    def reduced_of(s, first_tap, sources, skip):
        def chunk(i, inner):
            first = i * step
            taps = [
                x4[s, f, pl.ds(first + kr, step)].reshape(step * cols2, 4 * ch1)
                for f in sources for kr in range(3)
            ]
            weight = w1[3 * first_tap : 3 * (first_tap + len(sources))].reshape(-1, 2 * ch1)
            acc = jnp.dot(
                jnp.concatenate(taps, axis=1), weight, preferred_element_type=F32
            ).reshape(step, cols2, 2 * ch1)
            if skip is not None:
                acc = acc + resid[s, skip, pl.ds(first, step)].astype(F32)
            row = first + lax.broadcasted_iota(jnp.int32, (step, 1, 1), 0)
            acc = jnp.where((row < rows) | has_down, acc, 0.0)
            stage_h[:, 0:cols2] = acc[:, :, 0:ch1]
            h3[pl.ds(first, step), :, 0 : 2 * ch1] = acc.astype(BF16)
            h3[pl.ds(first, step), :, 2 * ch1 : 3 * ch1] = stage_h[:, 1 : cols2 + 1].astype(BF16)
            return inner

        lax.fori_loop(0, chunks, chunk, 0)
        taps = [
            jnp.concatenate([h3[2 * i + p] for i in range(rows2)], axis=0) for p in range(3)
        ]
        return jnp.dot(
            jnp.concatenate(taps, axis=1), wd[...].reshape(-1, ch2), preferred_element_type=F32
        ).reshape(rows2, cols2, ch2)

    def first_section(f):
        first_tap = max(0, 2 - f)
        sources = range(f + first_tap - 2, f + 1)
        if f < 2:
            arrive(first_moves[f])

        def slot(s):
            value = reduced_of(s, first_tap, sources, f)
            if f < 2:
                value = value + parr[f][pairing[0, s]].astype(F32)
            value = value.astype(BF16)
            red[f, s] = value
            gbuf[f, s, 1 : rows2 + 1] = silu(value.astype(F32)).astype(BF16)

        each_slot(slot)
        for item in gated_rows[f]:
            start(item)

    def first_partial(e):
        @pl.when(has_next)
        def _():
            def slot(s):
                value = reduced_of(s, 0, range(frames + e - 2, frames), None)
                pbuf[e, s] = value.astype(BF16)

            each_slot(slot)

        start(first_moves[e])

    def spread_gated(f):
        for item in gated_rows[f]:
            arrive(item)

        def slot(s):
            v = gbuf[f, s]
            stage_g[:, 8 : cols2 + 8] = v.astype(F32)
            g3[s, f, :, :, ch2 : 2 * ch2] = v
            g3[s, f, :, :, 0:ch2] = stage_g[:, 7 : cols2 + 7].astype(BF16)
            g3[s, f, :, :, 2 * ch2 : 3 * ch2] = stage_g[:, 9 : cols2 + 9].astype(BF16)

        each_slot(slot)

    def convolved(s, first_tap, sources):
        taps = [
            g3[s, f, kr : kr + rows2].reshape(rows2 * cols2, 3 * ch2)
            for f in sources for kr in range(3)
        ]
        weight = w2[3 * first_tap : 3 * (first_tap + len(sources))].reshape(-1, ch2)
        return jnp.dot(
            jnp.concatenate(taps, axis=1), weight, preferred_element_type=F32
        ).reshape(rows2, cols2, ch2)

    stores = [
        pltpu.make_async_copy(obuf.at[f], out.at[:, f], local_sem.at[5 + f]) for f in range(frames)
    ]

    def second_section(f):
        first_tap = max(0, 2 - f)
        sources = range(f + first_tap - 2, f + 1)

        def slot(s):
            value = red[f, s].astype(F32) + convolved(s, first_tap, sources)
            if f < 2:
                oacc[f, s] = value
            else:
                obuf[f, s] = value.astype(BF16)

        each_slot(slot)
        if f >= 2:
            stores[f].start()

    def second_partial(e):
        @pl.when(has_next)
        def _():
            def slot(s):
                qbuf[e, s] = convolved(s, 0, range(frames + e - 2, frames)).astype(BF16)

            each_slot(slot)

        start(second_moves[e])

    def finish(f):
        arrive(second_moves[f])

        def slot(s):
            obuf[f, s] = (oacc[f, s] + qarr[f][pairing[0, s]].astype(F32)).astype(BF16)

        each_slot(slot)
        stores[f].start()

    loads[0].wait()
    for item in own_rows:
        arrive(item)
    spread_own(frames - 1)
    for load in loads[1:4]:
        load.wait()
    first_partial(1)
    spread_own(frames - 2)
    first_partial(0)
    for f in range(frames - 2):
        spread_own(f)
    first_section(frames - 1)
    first_section(frames - 2)
    loads[4].wait()
    spread_gated(frames - 1)
    second_partial(1)
    spread_gated(frames - 2)
    second_partial(0)
    for f in range(frames - 3, -1, -1):
        first_section(f)
    for f in range(frames - 3, 0, -1):
        spread_gated(f)
    for f in range(frames - 1, 2, -1):
        second_section(f)
    spread_gated(0)
    for f in range(2, -1, -1):
        second_section(f)
    finish(1)
    finish(0)
    for copy, sends in sent:
        @pl.when(sends)
        def _():
            copy.wait_send()
    for store in stores:
        store.wait()


def on_device(n_tm, n_dom, video_group, pairing, weight_one, weight_down, weight_two):
    slots, frames, rows, width, ch1 = video_group.shape
    ch2 = weight_two.shape[-1]
    rows2, cols2 = rows // 2, width // 2
    step = chunk_rows(rows + 1, cols2, 512)
    any_spec = pl.BlockSpec(memory_space=pl.ANY)
    copies = 2 + 2 * frames + 4
    return pl.pallas_call(
        functools.partial(kernel, n_tm, n_dom),
        out_shape=jax.ShapeDtypeStruct((slots, frames, rows2, cols2, ch2), BF16),
        in_specs=[any_spec, pl.BlockSpec(memory_space=pltpu.SMEM), any_spec, any_spec, any_spec],
        out_specs=any_spec,
        scratch_shapes=[
            pltpu.VMEM((slots, frames, rows + 3, width, ch1), BF16),
            pltpu.VMEM((slots, frames, rows + 3, cols2, 4 * ch1), BF16),
            pltpu.VMEM((slots, frames, rows + 1, cols2, 2 * ch1), BF16),
            pltpu.VMEM((9, 4 * ch1, 2 * ch1), BF16),
            pltpu.VMEM((3, 3 * ch1, ch2), BF16),
            pltpu.VMEM((9, 3 * ch2, ch2), BF16),
            pltpu.VMEM((rows + 3, width + 16, ch1), F32),
            pltpu.VMEM((rows + 1, width, ch1), F32),
            pltpu.VMEM((rows + 1, cols2, 3 * ch1), BF16),
            pltpu.VMEM((step, cols2 + 8, ch1), F32),
            pltpu.VMEM((frames, slots, rows2, cols2, ch2), BF16),
            pltpu.VMEM((frames, slots, rows2 + 2, cols2, ch2), BF16),
            pltpu.VMEM((slots, frames, rows2 + 2, cols2, 3 * ch2), BF16),
            pltpu.VMEM((rows2 + 2, cols2 + 16, ch2), F32),
            pltpu.VMEM((frames, slots, rows2, cols2, ch2), BF16),
            pltpu.VMEM((2, slots, rows2, cols2, ch2), F32),
            pltpu.VMEM((2, slots, rows2, cols2, ch2), BF16),
            pltpu.VMEM((slots, rows2, cols2, ch2), BF16),
            pltpu.VMEM((slots, rows2, cols2, ch2), BF16),
            pltpu.VMEM((2, slots, rows2, cols2, ch2), BF16),
            pltpu.VMEM((slots, rows2, cols2, ch2), BF16),
            pltpu.VMEM((slots, rows2, cols2, ch2), BF16),
            pltpu.SemaphoreType.DMA((5 + frames,)),
            pltpu.SemaphoreType.DMA((copies,)),
            pltpu.SemaphoreType.DMA((copies,)),
        ],
        compiler_params=pltpu.CompilerParams(
            collective_id=0, has_side_effects=True, vmem_limit_bytes=63 * 1024 * 1024
        ),
        name="block",
    )(
        video_group,
        pairing,
        weight_one.reshape(9, 3 * ch1, ch1),
        weight_down.reshape(3, 3 * ch1, ch2),
        weight_two.reshape(9, 3 * ch2, ch2),
    )


def solution(mesh):
    return jax.shard_map(
        functools.partial(on_device, mesh.shape["tm"], mesh.shape["dom"]),
        mesh=mesh,
        in_specs=(P(None, "tm", "dom", None, None), P("tm", None), P(), P(), P()),
        out_specs=P(None, "tm", "dom", None, None),
        check_vma=False,
    )
```
